32 devices in a mesh: groups: 2 (over x), modes: 16 (over z, y, core).
Axes of the slice: x: 2, y: 2, z: 4, core: 2. Of those that a mesh axis runs over, the one named last changes fastest.
Arguments:
- mode_fields: bfloat16 [256, 256, 2048], P(('groups', 'modes')), parts along dimension 0, may hold values from -0.59765625 to 0.59765625
- coeff: float32 [256], P('groups'), parts along dimension 0, may hold values from -6 to 6
- eigen: float32 [256], P('groups'), parts along dimension 0, may hold values from 0.1 to 100
- map_friction: float32 [512, 2048], P(('groups', 'modes')), parts along dimension 0, may hold values from 1 to 2.5
- bed: float32 [512, 2048], P(('groups', 'modes')), parts along dimension 0, may hold values from -5 to 5
- smb: float32 [512, 2048], P(('groups', 'modes')), parts along dimension 0, may hold values from -0.6 to 0.4
- thickness: float32 [512, 2048], P(('groups', 'modes')), parts along dimension 0, may hold values from 1.9 to 2.6
Outputs:
- log_friction: float32 [512, 2048], P(('groups', 'modes')), parts along dimension 0
- final_thickness: float32 [512, 2048], P(('groups', 'modes')), parts along dimension 0
The draws below stay inside these ranges and needn't reach their ends.
There are 2 independent parts, one for each index of `groups`. The reference program is written for one: setup_inputs(seed, part) draws one part's arguments, and reference() takes and returns one part's arrays. A program takes and returns all parts, laid end to end along the dimension named above; each array names one. Nothing has to cross between parts.
All inputs are finite; a program needn't handle non-finite values.
Results may differ from the reference program's by a relative error of at most 0.0014.
Values may be sent and summed in bfloat16 or wider, within the bound.
A program may use at most 64 MiB of HBM per device.

```python
import math
import jax
import jax.numpy as jnp

MODES = 128
NY = 2048
STEPS = 8
NX = 256


def draw_bed(key, part):
    key_list = jax.random.split(jax.random.fold_in(key, 17), 2)
    phase_pair = jax.random.uniform(key_list[0], (2,), jnp.float32, 0.0, 2.0 * math.pi)
    row_index = jnp.arange(NX, dtype=jnp.float32)[:, None]
    column_index = jnp.arange(NY, dtype=jnp.float32)[None, :]
    wave_number = 2.0 * math.pi / 48.0
    amplitude = 2.0
    roughness = jnp.clip(0.25 * jax.random.normal(key_list[1], (NX, NY), jnp.float32), -0.75, 0.75)
    smooth_part = amplitude * (jnp.sin(wave_number * row_index + phase_pair[0]) + jnp.sin(wave_number * column_index + phase_pair[1]))
    return (smooth_part + roughness).astype(jnp.float32)


def with_spikes(drawn, stream_key, source, target, parts, factor):
    owner, partner = [(jnp.arange(drawn.shape[axis_at]) // (drawn.shape[axis_at] // parts)).reshape([-1 if axis == axis_at else 1 for axis in range(drawn.ndim)]) for axis_at in (source, target)]
    chosen = jax.random.permutation(stream_key, parts)[partner]
    strong = (owner == chosen) | (owner == (partner + parts // 2) % parts)
    return jnp.where(strong, factor * drawn, drawn)


def block_scale(own_key, extent, cuts, smallest, largest):
    level, own = 1.0, jax.random.fold_in(own_key, 6)
    for position, parts in cuts:
        heights = jnp.exp(jax.random.uniform(jax.random.fold_in(own, position), (parts,), jnp.float32, smallest / len(cuts), largest / len(cuts)))
        level = level * jnp.repeat(heights, extent[position] // parts).reshape([-1 if axis == position else 1 for axis in range(len(extent))])
    return level


def centred(stream_key, extent, width, most, cuts=(), kind=jnp.bfloat16):
    gain = block_scale(stream_key, extent, cuts, -0.22, 0.18) if cuts else 1.0
    drawn = jax.random.normal(stream_key, extent, jnp.float32) * width * gain
    return jnp.minimum(jnp.maximum(drawn, -most), most).astype(kind)


def bell_draw_with(stream_key, dims, deviation, reach, cuts, heavy, kind=jnp.bfloat16):
    drawn = deviation * jax.random.normal(stream_key, dims, jnp.float32)
    if cuts:
        drawn = drawn * block_scale(stream_key, dims, cuts, -0.22, 0.18)
    return jnp.clip(with_spikes(drawn, jax.random.fold_in(stream_key, 3), *heavy), -reach, reach).astype(kind)


def setup_inputs(seed: int = 0, part: int = 0) -> dict:
    streams_of = jax.random.split(jax.random.key(seed), 8)
    part_splits = jax.random.split(jax.random.fold_in(streams_of[7], part), 8)
    return {
        "mode_fields": bell_draw_with(part_splits[0], (MODES, NX, NY), 0.1, 0.59765625, ((0, 16),), (0, 1, 16, 2.0)),
        "coeff": centred(part_splits[1], (MODES,), 1.0, 6.0, (), jnp.float32),
        "eigen": jnp.clip(jnp.exp(jax.random.uniform(part_splits[2], (MODES,), jnp.float32, math.log(0.1), math.log(100.0))), 0.1, 100.0),
        "map_friction": jnp.clip(1.0 + 1.5 * jax.random.uniform(part_splits[3], (NX, NY), jnp.float32) ** block_scale(part_splits[3], (NX, NY), ((0, 16),), -0.2, 0.2), 1.0, 2.5),
        "bed": draw_bed(jax.random.fold_in(jax.random.fold_in(streams_of[7], part), 71), part),
        "smb": jnp.clip(-0.6 + 1 * jax.random.uniform(part_splits[5], (NX, NY), jnp.float32) ** block_scale(part_splits[5], (NX, NY), ((0, 16),), -0.2, 0.2), -0.6, 0.4),
        "thickness": jnp.clip(1.9 + 0.6999999 * jax.random.uniform(part_splits[6], (NX, NY), jnp.float32) ** block_scale(part_splits[6], (NX, NY), ((0, 16),), -0.2, 0.2), 1.9, 2.6),
    }


flow_rate = 0.02
slide_rate = 0.1
diff_cap = 0.5
time_step = 0.4

def advance(height, base, friction, balance):
    hpad = jnp.pad(height, ((0, 0), (2, 2)))
    bpad = jnp.pad(base, ((0, 0), (2, 2)))
    fpad = jnp.pad(friction, ((0, 0), (2, 2)))
    surface = bpad + hpad
    grad_x = (surface[2:, 1:-1] - surface[:-2, 1:-1]) * 0.5
    grad_y = (surface[1:-1, 2:] - surface[1:-1, :-2]) * 0.5
    center = hpad[1:-1, 1:-1]
    fcent = fpad[1:-1, 1:-1]
    squared = center * center
    diff = flow_rate * squared * squared * center * (grad_x * grad_x + grad_y * grad_y)
    diff = jnp.minimum(diff + slide_rate * squared * jnp.exp(-fcent), diff_cap)
    scent = surface[1:-1, 1:-1]
    mid_d = diff[1:-1, 1:-1]
    mid_s = scent[1:-1, 1:-1]
    up_x = 0.5 * (diff[2:, 1:-1] + mid_d) * (scent[2:, 1:-1] - mid_s)
    down_x = 0.5 * (mid_d + diff[:-2, 1:-1]) * (mid_s - scent[:-2, 1:-1])
    up_y = 0.5 * (diff[1:-1, 2:] + mid_d) * (scent[1:-1, 2:] - mid_s)
    down_y = 0.5 * (mid_d + diff[1:-1, :-2]) * (mid_s - scent[1:-1, :-2])
    total = up_x - down_x + up_y - down_y
    return jnp.maximum(height[2:-2] + time_step * (total + balance[2:-2]), 0.0)

def reference(mode_fields, coeff, eigen, map_friction, bed, smb, thickness):
    weights = (coeff / jnp.sqrt(1.0 + eigen)).astype(jnp.bfloat16)
    flat = mode_fields.reshape(MODES, NX * NY)
    perturb = jnp.dot(weights[None, :], flat, preferred_element_type=jnp.float32).reshape(NX, NY)
    log_friction = map_friction + perturb
    rim = ((2, 2), (0, 0))
    base = jnp.pad(bed, rim)
    friction = jnp.pad(log_friction, rim)
    balance = jnp.pad(smb, rim)
    height = thickness
    for step in range(STEPS):
        height = advance(jnp.pad(height, rim), base, friction, balance)
    return (log_friction, height)
```

```python
import functools

import jax
import jax.numpy as jnp
from jax import lax
from jax.experimental import pallas as pl
from jax.experimental.pallas import tpu as pltpu
from jax.sharding import PartitionSpec as P

STEPS = 8

flow_rate = 0.02
slide_rate = 0.1
diff_cap = 0.5
time_step = 0.4

WIRE = jnp.bfloat16
PAD = 8
F32 = jnp.float32


def kernel(
    n,
    coeff_ref, eigen_ref, map_ref, bed_ref, smb_ref, h0_ref, fields_ref,
    logf_ref, final_ref,
    mf, p1out, p1own, p1in, s2out, s2in, s3out, s3in, acc,
    st_out, st_in, h_in, f_out, f_in,
    ext_b, ext_e, ext_m, ext_h, ext_d, ext_s0, ext_s1,
    mf_sem, p1s, p1r, s2s, s2r, s3s, s3r, hs, hr,
):
    me = lax.axis_index("modes")
    c = me % 2
    a = (me // 2) % 2
    b = me // 4
    B = n // 4
    mode_dev = fields_ref.shape[0]
    rows, cols = map_ref.shape
    ks = list(range(1, B)) + [0]

    def bk(k):
        return lax.rem(b + k, B)

    def dest(k, aa, cc):
        return (bk(k) * 2 + aa) * 2 + cc

    order = [(k, aa, cc) for aa in (1, 0) for k in ks for cc in (1, 0)]

    def dest_of(k, aa, cc):
        return dest(k, a + aa - 2 * a * aa, c + cc - 2 * c * cc)

    def load(i):
        k, aa, cc = order[i]
        rr = pl.ds(pl.multiple_of(dest_of(k, aa, cc) * rows, rows), rows)
        return pltpu.make_async_copy(fields_ref.at[:, rr, :], mf.at[:, pl.ds(i * rows, rows), :], mf_sem.at[i])

    for i in range(n):
        load(i).start()

    left, right = lax.rem(me + n - 1, n), lax.rem(me + 1, n)
    core_peer = me + 1 - 2 * c
    y_peer = me + 2 - 4 * a
    barrier = pltpu.get_barrier_semaphore()

    def z_peer(k):
        return dest(k, a, c)

    for peer in [left, right, core_peer, y_peer] + [z_peer(k) for k in range(1, B)]:
        pl.semaphore_signal(barrier, inc=1, device_id={"modes": peer}, device_id_type=pl.DeviceIdType.MESH)

    w = coeff_ref[...] / jnp.sqrt(1.0 + eigen_ref[...])
    w = w.astype(jnp.bfloat16).astype(F32)
    lane = lax.broadcasted_iota(jnp.int32, w.shape, 1)
    ws = []
    for j in range(mode_dev):
        picked = jnp.where(lane == me * mode_dev + j, w, 0.0)
        ws.append(jnp.sum(picked, axis=1, keepdims=True))
    st_out[0] = bed_ref[...].astype(jnp.bfloat16)
    st_out[1] = smb_ref[...].astype(jnp.bfloat16)

    pl.semaphore_wait(barrier, 4 + B - 1)

    def remote(src, dst, ssem, rsem, peer):
        return pltpu.make_async_remote_copy(
            src_ref=src, dst_ref=dst, send_sem=ssem, recv_sem=rsem,
            device_id={"modes": peer}, device_id_type=pl.DeviceIdType.MESH)

    def halo(kind, side):
        src = (st_out, h0_ref, f_out)[kind]
        dst = (st_in, h_in, f_in)[kind]
        peer = right if side == 0 else left
        at = kind * 2 + side
        return remote(src, dst.at[side], hs.at[at], hr.at[at], peer)

    has_up, has_down = me > 0, me < n - 1

    def start_halo(kind):
        @pl.when(has_down)
        def _():
            halo(kind, 0).start()

        @pl.when(has_up)
        def _():
            halo(kind, 1).start()

    def wait_halo(kind):
        @pl.when(has_down)
        def _():
            halo(kind, 0).wait_send()
            halo(kind, 1).wait_recv()

        @pl.when(has_up)
        def _():
            halo(kind, 1).wait_send()
            halo(kind, 0).wait_recv()

    start_halo(1)
    start_halo(0)

    CT = min(512, cols)

    def col_loop(body):
        def step(j, carry):
            body(pl.ds(pl.multiple_of(j * CT, CT), CT))
            return carry
        lax.fori_loop(0, cols // CT, step, 0)

    def partial(i, out):
        load(i).wait()

        def body(cs):
            tot = None
            for j in range(mode_dev):
                term = mf[j, pl.ds(i * rows, rows), cs].astype(F32) * ws[j]
                tot = term if tot is None else tot + term
            out[:, cs] = tot
        col_loop(body)

    def s1copy(m):
        return remote(p1out.at[m], p1in.at[m], p1s.at[m], p1r.at[m], core_peer)

    def stage1(m):
        partial(2 * m, p1out.at[m])
        s1copy(m).start()
        partial(2 * m + 1, p1own.at[m])

    def s2copy(q):
        return remote(s2out.at[q], s2in.at[q], s2s.at[q], s2r.at[q], y_peer)

    def stage2(q):
        s1copy(q).wait_recv()

        def body(cs):
            s2out[q, :, cs] = (p1own[q, :, cs] + p1in[q, :, cs]).astype(WIRE)
        col_loop(body)
        s2copy(q).start()

    def s3copy(q):
        return remote(s3out.at[q], s3in.at[q], s3s.at[q], s3r.at[q], z_peer(ks[q]))

    def stage3(q):
        m = B + q
        s1copy(m).wait_recv()
        s2copy(q).wait_recv()

        def body(cs):
            tot = p1own[m, :, cs] + p1in[m, :, cs] + s2in[q, :, cs].astype(F32)
            if ks[q]:
                s3out[q, :, cs] = tot.astype(WIRE)
            else:
                acc[:, cs] = tot + map_ref[:, cs]
        col_loop(body)
        if ks[q]:
            s3copy(q).start()

    for q in range(B):
        stage1(q)
        if q:
            stage2(q - 1)
    stage1(B)
    stage2(B - 1)
    for q in range(1, B):
        stage1(B + q)
    for q in range(B):
        stage3(q)
    for q in range(B - 1):
        s3copy(q).wait_recv()

    def finish(cs):
        tot = acc[:, cs]
        for q in range(B - 1):
            tot = tot + s3in[q, :, cs].astype(F32)
        logf_ref[:, cs] = tot
        f_out[:, cs] = tot.astype(jnp.bfloat16)
    col_loop(finish)
    start_halo(2)

    top, mid, low = pl.ds(PAD, rows), pl.ds(PAD + rows, rows), pl.ds(PAD + 2 * rows, rows)
    zeros = jnp.zeros((rows, cols), F32)
    for ref in (ext_s0, ext_s1, ext_d, ext_h):
        ref[pl.ds(0, PAD), :] = jnp.zeros((PAD, cols), F32)
        ref[pl.ds(PAD + 3 * rows, PAD), :] = jnp.zeros((PAD, cols), F32)

    ext_b[mid, :] = bed_ref[...]
    ext_m[mid, :] = time_step * smb_ref[...]
    ext_h[mid, :] = h0_ref[...]
    ext_s0[mid, :] = bed_ref[...] + h0_ref[...]
    ext_e[mid, :] = slide_rate * jnp.exp(-logf_ref[...])
    wait_halo(0)
    wait_halo(1)

    def fill(side, where, present):
        @pl.when(present)
        def _():
            bb = st_in[side, 0].astype(F32)
            ext_b[where, :] = bb
            ext_m[where, :] = time_step * st_in[side, 1].astype(F32)
            hh = h_in[side]
            ext_h[where, :] = hh
            ext_s0[where, :] = bb + hh

        @pl.when(jnp.logical_not(present))
        def _():
            for ref in (ext_h, ext_s0, ext_s1, ext_d):
                ref[where, :] = zeros
    fill(0, top, has_up)
    fill(1, low, has_down)
    wait_halo(2)

    def fill_e(side, where, present):
        @pl.when(present)
        def _():
            ext_e[where, :] = slide_rate * jnp.exp(-f_in[side].astype(F32))
    fill_e(0, top, has_up)
    fill_e(1, low, has_down)

    for m in range(2 * B):
        s1copy(m).wait_send()
    for q in range(B):
        s2copy(q).wait_send()
        if ks[q]:
            s3copy(q).wait_send()

    col = lax.broadcasted_iota(jnp.int32, (8, cols), 1)
    first_col, last_col = col == 0, col == cols - 1

    def before(v):
        return jnp.where(first_col, 0.0, pltpu.roll(v, 1, 1))

    def after(v):
        return jnp.where(last_col, 0.0, pltpu.roll(v, cols - 1, 1))

    row = lax.broadcasted_iota(jnp.int32, (8, cols), 0)
    first_row, last_row = row == 0, row == 7

    def above(ref, r, v):
        prev = ref[pl.ds(pl.multiple_of(r - 8, 8), 8), :]
        return pltpu.roll(jnp.where(last_row, prev, v), 1, 0)

    def below(ref, r, v):
        following = ref[pl.ds(pl.multiple_of(r + 8, 8), 8), :]
        return pltpu.roll(jnp.where(first_row, following, v), 7, 0)

    blocks = rows // 8
    lowest = jnp.where(has_up, 0, blocks)
    highest = jnp.where(has_down, 3 * blocks, 2 * blocks)
    total = 3 * rows
    margin = rows - 2 * STEPS

    for t in range(1, STEPS + 1):
        s_ref, s_new = (ext_s0, ext_s1) if t % 2 else (ext_s1, ext_s0)
        lo_h = margin + 2 * t
        lo_d = lo_h - 1

        def d_block(i, carry):
            r = PAD + i * 8
            here = pl.ds(pl.multiple_of(r, 8), 8)
            s = s_ref[here, :]
            gx = below(s_ref, r, s) - above(s_ref, r, s)
            gy = after(s) - before(s)
            h = ext_h[here, :]
            sq = h * h
            d = (0.25 * flow_rate) * (sq * sq * h) * (gx * gx + gy * gy) + sq * ext_e[here, :]
            ext_d[here, :] = jnp.minimum(d, diff_cap)
            return carry

        def h_block(i, carry):
            r = PAD + i * 8
            here = pl.ds(pl.multiple_of(r, 8), 8)
            s, d = s_ref[here, :], ext_d[here, :]
            div = (below(ext_d, r, d) + d) * (below(s_ref, r, s) - s)
            div += (above(ext_d, r, d) + d) * (above(s_ref, r, s) - s)
            div += (after(d) + d) * (after(s) - s)
            div += (before(d) + d) * (before(s) - s)
            h = jnp.maximum(ext_h[here, :] + ((0.5 * time_step) * div + ext_m[here, :]), 0.0)
            if t < STEPS:
                ext_h[here, :] = h
                s_new[here, :] = ext_b[here, :] + h
            else:
                final_ref[pl.ds(pl.multiple_of(i * 8 - rows, 8), 8), :] = h
            return carry

        lax.fori_loop(jnp.maximum(lowest, lo_d // 8), jnp.minimum(highest, -(-(total - lo_d) // 8)), d_block, 0)
        lax.fori_loop(jnp.maximum(lowest, lo_h // 8), jnp.minimum(highest, -(-(total - lo_h) // 8)), h_block, 0)


def per_device(n, mode_fields, coeff, eigen, map_friction, bed, smb, thickness):
    rows, cols = map_friction.shape
    mode_dev = mode_fields.shape[0]
    B = n // 4
    modes = coeff.shape[0]
    vmem = pl.BlockSpec(memory_space=pltpu.VMEM)
    strip = (rows, cols)
    ext = (3 * rows + 2 * PAD, cols)
    bf = jnp.bfloat16
    dma = pltpu.SemaphoreType.DMA
    return pl.pallas_call(
        functools.partial(kernel, n),
        out_shape=(jax.ShapeDtypeStruct(strip, F32),) * 2,
        in_specs=[vmem] * 6 + [pl.BlockSpec(memory_space=pl.ANY)],
        out_specs=(vmem, vmem),
        scratch_shapes=[
            pltpu.VMEM((mode_dev, n * rows, cols), bf),
            pltpu.VMEM((2 * B,) + strip, F32),
            pltpu.VMEM((2 * B,) + strip, F32),
            pltpu.VMEM((2 * B,) + strip, F32),
            pltpu.VMEM((B,) + strip, WIRE),
            pltpu.VMEM((B,) + strip, WIRE),
            pltpu.VMEM((B,) + strip, WIRE),
            pltpu.VMEM((B,) + strip, WIRE),
            pltpu.VMEM(strip, F32),
            pltpu.VMEM((2,) + strip, bf),
            pltpu.VMEM((2, 2) + strip, bf),
            pltpu.VMEM((2,) + strip, F32),
            pltpu.VMEM(strip, bf),
            pltpu.VMEM((2,) + strip, bf),
        ] + [pltpu.VMEM(ext, F32)] * 7 + [
            dma((n,)), dma((2 * B,)), dma((2 * B,)), dma((B,)), dma((B,)), dma((B,)), dma((B,)), dma((6,)), dma((6,)),
        ],
        compiler_params=pltpu.CompilerParams(collective_id=0, has_side_effects=True, vmem_limit_bytes=60 * 2**20),
        name="posterior_ice",
    )(coeff.reshape(1, modes), eigen.reshape(1, modes), map_friction, bed, smb, thickness, mode_fields)


def solution(mesh):
    n = mesh.shape["modes"]
    return jax.shard_map(
        functools.partial(per_device, n),
        mesh=mesh,
        in_specs=(
            P(("groups", "modes"), None, None),
            P("groups"),
            P("groups"),
            P(("groups", "modes"), None),
            P(("groups", "modes"), None),
            P(("groups", "modes"), None),
            P(("groups", "modes"), None),
        ),
        out_specs=(P(("groups", "modes"), None), P(("groups", "modes"), None)),
        check_vma=False,
    )
```

```python
import functools

import jax
import jax.numpy as jnp
from jax import lax
from jax.experimental import pallas as pl
from jax.experimental.pallas import tpu as pltpu
from jax.sharding import PartitionSpec as P

STEPS = 8

flow_rate = 0.02
slide_rate = 0.1
diff_cap = 0.5
time_step = 0.4

WIRE = jnp.bfloat16
PAD = 8
LANES = 128
GROUP = 4
F32 = jnp.float32


def kernel(
    n,
    coeff_hbm, eigen_hbm, map_hbm, bed_hbm, smb_hbm, h0_hbm, fields_ref,
    logf_hbm, final_hbm,
    coeff_ref, eigen_ref, map_ref, bed_ref, smb_ref, h0_ref, logf_ref, final_ref, in_sem, out_sem,
    mf, p1out, p1own, p1in, s2out, s2in, s3out, s3in, acc,
    st_out, st_in, f_out, f_in,
    ext_b, ext_e, ext_m, ext_h, ext_d, ext_g, ext_s0, ext_s1,
    mf_sem, p1s, p1r, s2s, s2r, s3s, s3r, hs, hr,
):
    me = lax.axis_index("modes")
    c = me % 2
    a = (me // 2) % 2
    b = me // 4
    B = n // 4
    mode_dev = fields_ref.shape[0]
    rows, cols = map_ref.shape
    ks = list(range(1, B)) + [0]

    def bk(k):
        return lax.rem(b + k, B)

    def dest(k, aa, cc):
        return (bk(k) * 2 + aa) * 2 + cc

    order = [(k, aa, cc) for aa in (1, 0) for k in ks for cc in (1, 0)]

    def dest_of(k, aa, cc):
        return dest(k, a + aa - 2 * a * aa, c + cc - 2 * c * cc)

    def load(i):
        k, aa, cc = order[i]
        rr = pl.ds(pl.multiple_of(dest_of(k, aa, cc) * rows, rows), rows)
        return pltpu.make_async_copy(fields_ref.at[:, rr, :], mf.at[:, pl.ds(i * rows, rows), :], mf_sem.at[i])

    hbm = (bed_hbm, smb_hbm, h0_hbm, coeff_hbm, eigen_hbm, map_hbm)
    own = (bed_ref, smb_ref, h0_ref, coeff_ref, eigen_ref, map_ref)
    takes = [pltpu.make_async_copy(x, y, in_sem.at[i]) for i, (x, y) in enumerate(zip(hbm, own))]
    gives = [pltpu.make_async_copy(x, y, out_sem.at[i]) for i, (x, y) in enumerate(((logf_ref, logf_hbm), (final_ref, final_hbm)))]
    for take in takes:
        take.start()
    for i in range(n):
        load(i).start()

    left, right = lax.rem(me + n - 1, n), lax.rem(me + 1, n)
    core_peer = me + 1 - 2 * c
    y_peer = me + 2 - 4 * a
    barrier = pltpu.get_barrier_semaphore()

    def z_peer(k):
        return dest(k, a, c)

    for peer in [left, right, core_peer, y_peer] + [z_peer(k) for k in range(1, B)]:
        pl.semaphore_signal(barrier, inc=1, device_id={"modes": peer}, device_id_type=pl.DeviceIdType.MESH)

    for take in takes:
        take.wait()
    w = coeff_ref[...] / jnp.sqrt(1.0 + eigen_ref[...])
    w = w.astype(jnp.bfloat16).astype(F32)
    lane = lax.broadcasted_iota(jnp.int32, w.shape, 1)
    ws = []
    for j in range(mode_dev):
        picked = jnp.where(lane == me * mode_dev + j, w, 0.0)
        ws.append(jnp.sum(picked, axis=1, keepdims=True))
    st_out[0] = bed_ref[...].astype(jnp.bfloat16)
    st_out[1] = smb_ref[...].astype(jnp.bfloat16)
    st_out[2] = h0_ref[...].astype(jnp.bfloat16)

    pl.semaphore_wait(barrier, 4 + B - 1)

    def remote(src, dst, ssem, rsem, peer):
        return pltpu.make_async_remote_copy(
            src_ref=src, dst_ref=dst, send_sem=ssem, recv_sem=rsem,
            device_id={"modes": peer}, device_id_type=pl.DeviceIdType.MESH)

    def halo(kind, side):
        src = (st_out, f_out)[kind]
        dst = (st_in, f_in)[kind]
        peer = right if side == 0 else left
        at = kind * 2 + side
        return remote(src, dst.at[side], hs.at[at], hr.at[at], peer)

    has_up, has_down = me > 0, me < n - 1

    def start_halo(kind):
        @pl.when(has_down)
        def _():
            halo(kind, 0).start()

        @pl.when(has_up)
        def _():
            halo(kind, 1).start()

    def wait_halo(kind):
        @pl.when(has_down)
        def _():
            halo(kind, 0).wait_send()
            halo(kind, 1).wait_recv()

        @pl.when(has_up)
        def _():
            halo(kind, 1).wait_send()
            halo(kind, 0).wait_recv()

    start_halo(0)

    CT = min(512, cols)

    def col_loop(body):
        def step(j, carry):
            body(pl.ds(pl.multiple_of(j * CT, CT), CT))
            return carry
        lax.fori_loop(0, cols // CT, step, 0)

    def partial(i, out):
        load(i).wait()

        def body(cs):
            tot = None
            for j in range(mode_dev):
                term = mf[j, pl.ds(i * rows, rows), cs].astype(F32) * ws[j]
                tot = term if tot is None else tot + term
            out[:, cs] = tot
        col_loop(body)

    def s1copy(m):
        return remote(p1out.at[m], p1in.at[m], p1s.at[m], p1r.at[m], core_peer)

    def stage1(m):
        partial(2 * m, p1out.at[m])
        s1copy(m).start()
        partial(2 * m + 1, p1own.at[m])

    def s2copy(q):
        return remote(s2out.at[q], s2in.at[q], s2s.at[q], s2r.at[q], y_peer)

    def stage2(q):
        s1copy(q).wait_recv()

        def body(cs):
            s2out[q, :, cs] = (p1own[q, :, cs] + p1in[q, :, cs]).astype(WIRE)
        col_loop(body)
        s2copy(q).start()

    def s3copy(q):
        return remote(s3out.at[q], s3in.at[q], s3s.at[q], s3r.at[q], z_peer(ks[q]))

    def stage3(q):
        m = B + q
        s1copy(m).wait_recv()
        s2copy(q).wait_recv()

        def body(cs):
            tot = p1own[m, :, cs] + p1in[m, :, cs] + s2in[q, :, cs].astype(F32)
            if ks[q]:
                s3out[q, :, cs] = tot.astype(WIRE)
            else:
                acc[:, cs] = tot + map_ref[:, cs]
        col_loop(body)
        if ks[q]:
            s3copy(q).start()

    for q in range(B):
        stage1(q)
        if q:
            stage2(q - 1)
    stage1(B)
    stage2(B - 1)
    for q in range(1, B):
        stage1(B + q)
    for q in range(B):
        stage3(q)
    for q in range(B - 1):
        s3copy(q).wait_recv()

    def finish(cs):
        tot = acc[:, cs]
        for q in range(B - 1):
            tot = tot + s3in[q, :, cs].astype(F32)
        logf_ref[:, cs] = tot
        f_out[:, cs] = tot.astype(jnp.bfloat16)
    col_loop(finish)
    start_halo(1)
    gives[0].start()

    tiles = cols // LANES
    top, mid, low = pl.ds(PAD, rows), pl.ds(PAD + rows, rows), pl.ds(PAD + 2 * rows, rows)
    whole = 3 * rows + 2 * PAD

    def clear(ref, where, size):
        for j in range(tiles):
            ref[j + 1, where, :] = jnp.zeros((size, LANES), F32)

    for ref in (ext_s0, ext_s1, ext_d):
        clear(ref, pl.ds(0, PAD), PAD)
        clear(ref, pl.ds(PAD + 3 * rows, PAD), PAD)
        for j in (0, tiles + 1):
            ref[j] = jnp.zeros((whole, LANES), F32)
    ext_g[0] = jnp.zeros((whole, LANES), F32)

    def lanes(j):
        return slice(j * LANES, (j + 1) * LANES)

    for j in range(tiles):
        bb, hh = bed_ref[:, lanes(j)], h0_ref[:, lanes(j)]
        ext_b[j + 1, mid, :] = bb
        ext_m[j + 1, mid, :] = time_step * smb_ref[:, lanes(j)]
        ext_h[j + 1, mid, :] = hh
        ext_s0[j + 1, mid, :] = bb + hh
        ext_e[j + 1, mid, :] = slide_rate * jnp.exp(-logf_ref[:, lanes(j)])
    wait_halo(0)

    def fill(side, where, present):
        @pl.when(present)
        def _():
            for j in range(tiles):
                bb = st_in[side, 0, :, lanes(j)].astype(F32)
                hh = st_in[side, 2, :, lanes(j)].astype(F32)
                ext_b[j + 1, where, :] = bb
                ext_m[j + 1, where, :] = time_step * st_in[side, 1, :, lanes(j)].astype(F32)
                ext_h[j + 1, where, :] = hh
                ext_s0[j + 1, where, :] = bb + hh

        @pl.when(jnp.logical_not(present))
        def _():
            for ref in (ext_s0, ext_s1, ext_d):
                clear(ref, where, rows)
    fill(0, top, has_up)
    fill(1, low, has_down)
    wait_halo(1)

    def fill_e(side, where, present):
        @pl.when(present)
        def _():
            for j in range(tiles):
                ext_e[j + 1, where, :] = slide_rate * jnp.exp(-f_in[side, :, lanes(j)].astype(F32))
    fill_e(0, top, has_up)
    fill_e(1, low, has_down)

    for m in range(2 * B):
        s1copy(m).wait_send()
    for q in range(B):
        s2copy(q).wait_send()
        if ks[q]:
            s3copy(q).wait_send()

    margin = rows - 2 * STEPS

    def sweep(first, last, body):
        for lo, hi, present in ((0, rows, has_up), (rows, 2 * rows, None), (2 * rows, 3 * rows, has_down)):
            lo, hi = max(lo, first // 8 * 8), min(hi, -(-last // 8) * 8)
            if lo >= hi:
                continue
            if present is None:
                body(PAD + lo, hi - lo)
            else:
                pl.when(present)(functools.partial(body, PAD + lo, hi - lo))

    for t in range(1, STEPS + 1):
        s_ref, s_new = (ext_s0, ext_s1) if t % 2 else (ext_s1, ext_s0)
        lo_h = margin + 2 * t

        lane = lax.broadcasted_iota(jnp.int32, (1, 8, LANES), 2)
        first_lane, last_lane = lane == 0, lane == LANES - 1

        def d_rows(r, size):
            for at in range(r, r + size, 8):
                here, up, down = (slice(at + o, at + o + 8) for o in (0, -1, 1))
                for j in range(1, tiles + 1, GROUP):
                    now, later, sooner = (slice(j + o, j + o + GROUP) for o in (0, 1, -1))
                    s = s_ref[now, here, :]
                    right = pltpu.roll(jnp.where(first_lane, s_ref[later, here, :], s), LANES - 1, 2)
                    left_ = pltpu.roll(jnp.where(last_lane, s_ref[sooner, here, :], s), 1, 2)
                    gx = s_ref[now, down, :] - s_ref[now, up, :]
                    gy = right - left_
                    h = ext_h[now, here, :]
                    sq = h * h
                    d = sq * ((0.25 * flow_rate) * (sq * h) * (gx * gx + gy * gy) + ext_e[now, here, :])
                    ext_d[now, here, :] = jnp.minimum(d, diff_cap)
                    ext_g[now, here, :] = right - s

        def h_rows(r, size):
            for at in range(r, r + size, 8):
                here, up, down = (slice(at + o, at + o + 8) for o in (0, -1, 1))
                edge = pltpu.roll(ext_d[1:2, here, :] * s_ref[1:2, here, :], LANES - 1, 2)
                for j in range(1, tiles + 1, GROUP):
                    now, later = (slice(j + o, j + o + GROUP) for o in (0, 1))
                    s, d = s_ref[now, here, :], ext_d[now, here, :]
                    right = pltpu.roll(jnp.where(first_lane, ext_d[later, here, :], d), LANES - 1, 2)
                    flux = (right + d) * ext_g[now, here, :]
                    sooner = jnp.concatenate([edge, flux[:-1]], axis=0)
                    edge = flux[-1:]
                    div = (ext_d[now, down, :] + d) * (s_ref[now, down, :] - s)
                    div += (ext_d[now, up, :] + d) * (s_ref[now, up, :] - s)
                    div += flux - pltpu.roll(jnp.where(last_lane, sooner, flux), 1, 2)
                    h = jnp.maximum(ext_h[now, here, :] + ((0.5 * time_step) * div + ext_m[now, here, :]), 0.0)
                    ext_h[now, here, :] = h
                    if t < STEPS:
                        s_new[now, here, :] = ext_b[now, here, :] + h

        sweep(lo_h - 1, 3 * rows - lo_h + 1, d_rows)
        sweep(lo_h, 3 * rows - lo_h, h_rows)

    for j in range(tiles):
        final_ref[:, lanes(j)] = ext_h[j + 1, mid, :]
    gives[1].start()
    gives[0].wait()
    gives[1].wait()


def per_device(n, mode_fields, coeff, eigen, map_friction, bed, smb, thickness):
    rows, cols = map_friction.shape
    mode_dev = mode_fields.shape[0]
    B = n // 4
    modes = coeff.shape[0]
    anywhere = pl.BlockSpec(memory_space=pl.ANY)
    strip = (rows, cols)
    ext = (cols // LANES + 2, 3 * rows + 2 * PAD, LANES)
    bf = jnp.bfloat16
    dma = pltpu.SemaphoreType.DMA
    return pl.pallas_call(
        functools.partial(kernel, n),
        out_shape=(jax.ShapeDtypeStruct(strip, F32),) * 2,
        in_specs=[anywhere] * 7,
        out_specs=(anywhere, anywhere),
        scratch_shapes=[
            pltpu.VMEM((1, modes), F32),
            pltpu.VMEM((1, modes), F32),
        ] + [pltpu.VMEM(strip, F32)] * 6 + [
            dma((6,)),
            dma((2,)),
            pltpu.VMEM((mode_dev, n * rows, cols), bf),
            pltpu.VMEM((2 * B,) + strip, F32),
            pltpu.VMEM((2 * B,) + strip, F32),
            pltpu.VMEM((2 * B,) + strip, F32),
            pltpu.VMEM((B,) + strip, WIRE),
            pltpu.VMEM((B,) + strip, WIRE),
            pltpu.VMEM((B,) + strip, WIRE),
            pltpu.VMEM((B,) + strip, WIRE),
            pltpu.VMEM(strip, F32),
            pltpu.VMEM((3,) + strip, bf),
            pltpu.VMEM((2, 3) + strip, bf),
            pltpu.VMEM(strip, bf),
            pltpu.VMEM((2,) + strip, bf),
        ] + [pltpu.VMEM(ext, F32)] * 8 + [
            dma((n,)), dma((2 * B,)), dma((2 * B,)), dma((B,)), dma((B,)), dma((B,)), dma((B,)), dma((4,)), dma((4,)),
        ],
        compiler_params=pltpu.CompilerParams(collective_id=0, has_side_effects=True, vmem_limit_bytes=60 * 2**20),
        name="posterior_ice",
    )(coeff.reshape(1, modes), eigen.reshape(1, modes), map_friction, bed, smb, thickness, mode_fields)


def solution(mesh):
    n = mesh.shape["modes"]
    return jax.shard_map(
        functools.partial(per_device, n),
        mesh=mesh,
        in_specs=(
            P(("groups", "modes"), None, None),
            P("groups"),
            P("groups"),
            P(("groups", "modes"), None),
            P(("groups", "modes"), None),
            P(("groups", "modes"), None),
            P(("groups", "modes"), None),
        ),
        out_specs=(P(("groups", "modes"), None), P(("groups", "modes"), None)),
        check_vma=False,
    )
```

```python
import functools

import jax
import jax.numpy as jnp
from jax import lax
from jax.experimental import pallas as pl
from jax.experimental.pallas import tpu as pltpu
from jax.sharding import PartitionSpec as P

STEPS = 8

flow_rate = 0.02
slide_rate = 0.1
diff_cap = 0.5
time_step = 0.4

WIRE = jnp.bfloat16
PAD = 8
LANES = 128
GROUP = 4
F32 = jnp.float32


def kernel(
    n,
    coeff_hbm, eigen_hbm, map_hbm, bed_hbm, smb_hbm, h0_hbm, fields_ref,
    logf_hbm, final_hbm,
    coeff_ref, eigen_ref, map_ref, bed_ref, smb_ref, h0_ref, logf_ref, final_ref, in_sem, out_sem,
    mf, p1out, p1own, p1in, s2out, s2in, s3out, s3in, acc,
    st_out, st_in, f_out, f_in,
    ext_b, ext_e, ext_m, ext_h, ext_d, ext_g, ext_s0, ext_s1,
    mf_sem, p1s, p1r, s2s, s2r, s3s, s3r, hs, hr,
):
    me = lax.axis_index("modes")
    c = me % 2
    a = (me // 2) % 2
    b = me // 4
    B = n // 4
    mode_dev = fields_ref.shape[0]
    rows, cols = map_ref.shape
    ks = list(range(1, B)) + [0]

    def bk(k):
        return lax.rem(b + k, B)

    def dest(k, aa, cc):
        return (bk(k) * 2 + aa) * 2 + cc

    order = [(k, aa, cc) for aa in (1, 0) for k in ks for cc in (1, 0)]

    def dest_of(k, aa, cc):
        return dest(k, a + aa - 2 * a * aa, c + cc - 2 * c * cc)

    def load(i):
        k, aa, cc = order[i]
        rr = pl.ds(pl.multiple_of(dest_of(k, aa, cc) * rows, rows), rows)
        return pltpu.make_async_copy(fields_ref.at[:, rr, :], mf.at[:, pl.ds(i * rows, rows), :], mf_sem.at[i])

    hbm = (bed_hbm, smb_hbm, h0_hbm, coeff_hbm, eigen_hbm, map_hbm)
    own = (bed_ref, smb_ref, h0_ref, coeff_ref, eigen_ref, map_ref)
    takes = [pltpu.make_async_copy(x, y, in_sem.at[i]) for i, (x, y) in enumerate(zip(hbm, own))]
    gives = [pltpu.make_async_copy(x, y, out_sem.at[i]) for i, (x, y) in enumerate(((logf_ref, logf_hbm), (final_ref, final_hbm)))]
    for take in takes:
        take.start()
    for i in range(n):
        load(i).start()

    left, right = lax.rem(me + n - 1, n), lax.rem(me + 1, n)
    core_peer = me + 1 - 2 * c
    y_peer = me + 2 - 4 * a
    barrier = pltpu.get_barrier_semaphore()

    def z_peer(k):
        return dest(k, a, c)

    for peer in [left, right, core_peer, y_peer] + [z_peer(k) for k in range(1, B)]:
        pl.semaphore_signal(barrier, inc=1, device_id={"modes": peer}, device_id_type=pl.DeviceIdType.MESH)

    for take in takes:
        take.wait()
    w = coeff_ref[...] / jnp.sqrt(1.0 + eigen_ref[...])
    w = w.astype(jnp.bfloat16).astype(F32)
    lane = lax.broadcasted_iota(jnp.int32, w.shape, 1)
    ws = []
    for j in range(mode_dev):
        picked = jnp.where(lane == me * mode_dev + j, w, 0.0)
        ws.append(jnp.sum(picked, axis=1, keepdims=True))
    st_out[0] = bed_ref[...].astype(jnp.bfloat16)
    st_out[1] = smb_ref[...].astype(jnp.bfloat16)
    st_out[2] = h0_ref[...].astype(jnp.bfloat16)

    pl.semaphore_wait(barrier, 4 + B - 1)

    def remote(src, dst, ssem, rsem, peer):
        return pltpu.make_async_remote_copy(
            src_ref=src, dst_ref=dst, send_sem=ssem, recv_sem=rsem,
            device_id={"modes": peer}, device_id_type=pl.DeviceIdType.MESH)

    def halo(kind, side):
        src = (st_out, f_out)[kind]
        dst = (st_in, f_in)[kind]
        peer = right if side == 0 else left
        at = kind * 2 + side
        return remote(src, dst.at[side], hs.at[at], hr.at[at], peer)

    has_up, has_down = me > 0, me < n - 1

    def start_halo(kind):
        @pl.when(has_down)
        def _():
            halo(kind, 0).start()

        @pl.when(has_up)
        def _():
            halo(kind, 1).start()

    def wait_halo(kind):
        @pl.when(has_down)
        def _():
            halo(kind, 0).wait_send()
            halo(kind, 1).wait_recv()

        @pl.when(has_up)
        def _():
            halo(kind, 1).wait_send()
            halo(kind, 0).wait_recv()


    CT = min(512, cols)

    def col_loop(body):
        def step(j, carry):
            body(pl.ds(pl.multiple_of(j * CT, CT), CT))
            return carry
        lax.fori_loop(0, cols // CT, step, 0)

    def partial(i, out):
        load(i).wait()

        def body(cs):
            tot = None
            for j in range(mode_dev):
                term = mf[j, pl.ds(i * rows, rows), cs].astype(F32) * ws[j]
                tot = term if tot is None else tot + term
            out[:, cs] = tot
        col_loop(body)

    def s1copy(m):
        return remote(p1out.at[m], p1in.at[m], p1s.at[m], p1r.at[m], core_peer)

    def stage1(m):
        partial(2 * m, p1out.at[m])
        s1copy(m).start()
        partial(2 * m + 1, p1own.at[m])

    def s2copy(q):
        return remote(s2out.at[q], s2in.at[q], s2s.at[q], s2r.at[q], y_peer)

    def stage2(q):
        s1copy(q).wait_recv()

        def body(cs):
            s2out[q, :, cs] = (p1own[q, :, cs] + p1in[q, :, cs]).astype(WIRE)
        col_loop(body)
        s2copy(q).start()

    def s3copy(q):
        return remote(s3out.at[q], s3in.at[q], s3s.at[q], s3r.at[q], z_peer(ks[q]))

    def stage3(q):
        m = B + q
        s1copy(m).wait_recv()
        s2copy(q).wait_recv()

        def body(cs):
            tot = p1own[m, :, cs] + p1in[m, :, cs] + s2in[q, :, cs].astype(F32)
            if ks[q]:
                s3out[q, :, cs] = tot.astype(WIRE)
            else:
                acc[:, cs] = tot + map_ref[:, cs]
        col_loop(body)
        if ks[q]:
            s3copy(q).start()

    for q in range(B):
        stage1(q)
        if q:
            stage2(q - 1)
    stage1(B)
    stage2(B - 1)
    for q in range(1, B):
        stage1(B + q)
    for q in range(B):
        stage3(q)
    start_halo(0)
    for q in range(B - 1):
        s3copy(q).wait_recv()

    def finish(cs):
        tot = acc[:, cs]
        for q in range(B - 1):
            tot = tot + s3in[q, :, cs].astype(F32)
        logf_ref[:, cs] = tot
        f_out[:, cs] = tot.astype(jnp.bfloat16)
    col_loop(finish)
    start_halo(1)
    gives[0].start()

    tiles = cols // LANES
    top, mid, low = pl.ds(PAD, rows), pl.ds(PAD + rows, rows), pl.ds(PAD + 2 * rows, rows)
    whole = 3 * rows + 2 * PAD

    def clear(ref, where, size):
        for j in range(tiles):
            ref[j + 1, where, :] = jnp.zeros((size, LANES), F32)

    for ref in (ext_s0, ext_s1, ext_d):
        clear(ref, pl.ds(0, PAD), PAD)
        clear(ref, pl.ds(PAD + 3 * rows, PAD), PAD)
        for j in (0, tiles + 1):
            ref[j] = jnp.zeros((whole, LANES), F32)
    ext_g[0] = jnp.zeros((whole, LANES), F32)

    def lanes(j):
        return slice(j * LANES, (j + 1) * LANES)

    for j in range(tiles):
        bb, hh = bed_ref[:, lanes(j)], h0_ref[:, lanes(j)]
        ext_b[j + 1, mid, :] = bb
        ext_m[j + 1, mid, :] = time_step * smb_ref[:, lanes(j)]
        ext_h[j + 1, mid, :] = hh
        ext_s0[j + 1, mid, :] = bb + hh
        ext_e[j + 1, mid, :] = slide_rate * jnp.exp(-logf_ref[:, lanes(j)])
    wait_halo(0)

    def fill(side, where, present):
        @pl.when(present)
        def _():
            for j in range(tiles):
                bb = st_in[side, 0, :, lanes(j)].astype(F32)
                hh = st_in[side, 2, :, lanes(j)].astype(F32)
                ext_b[j + 1, where, :] = bb
                ext_m[j + 1, where, :] = time_step * st_in[side, 1, :, lanes(j)].astype(F32)
                ext_h[j + 1, where, :] = hh
                ext_s0[j + 1, where, :] = bb + hh

        @pl.when(jnp.logical_not(present))
        def _():
            for ref in (ext_s0, ext_s1, ext_d):
                clear(ref, where, rows)
    fill(0, top, has_up)
    fill(1, low, has_down)
    wait_halo(1)

    def fill_e(side, where, present):
        @pl.when(present)
        def _():
            for j in range(tiles):
                ext_e[j + 1, where, :] = slide_rate * jnp.exp(-f_in[side, :, lanes(j)].astype(F32))
    fill_e(0, top, has_up)
    fill_e(1, low, has_down)

    for m in range(2 * B):
        s1copy(m).wait_send()
    for q in range(B):
        s2copy(q).wait_send()
        if ks[q]:
            s3copy(q).wait_send()

    margin = rows - 2 * STEPS

    def sweep(first, last, body):
        for lo, hi, present in ((0, rows, has_up), (rows, 2 * rows, None), (2 * rows, 3 * rows, has_down)):
            lo, hi = max(lo, first // 8 * 8), min(hi, -(-last // 8) * 8)
            if lo >= hi:
                continue
            if present is None:
                body(PAD + lo, hi - lo)
            else:
                pl.when(present)(functools.partial(body, PAD + lo, hi - lo))

    for t in range(1, STEPS + 1):
        s_ref, s_new = (ext_s0, ext_s1) if t % 2 else (ext_s1, ext_s0)
        lo_h = margin + 2 * t

        lane = lax.broadcasted_iota(jnp.int32, (1, 8, LANES), 2)
        first_lane, last_lane = lane == 0, lane == LANES - 1

        def d_rows(r, size):
            for at in range(r, r + size, 8):
                here, up, down = (slice(at + o, at + o + 8) for o in (0, -1, 1))
                for j in range(1, tiles + 1, GROUP):
                    now, later, sooner = (slice(j + o, j + o + GROUP) for o in (0, 1, -1))
                    s = s_ref[now, here, :]
                    right = pltpu.roll(jnp.where(first_lane, s_ref[later, here, :], s), LANES - 1, 2)
                    left_ = pltpu.roll(jnp.where(last_lane, s_ref[sooner, here, :], s), 1, 2)
                    gx = s_ref[now, down, :] - s_ref[now, up, :]
                    gy = right - left_
                    h = ext_h[now, here, :]
                    sq = h * h
                    d = sq * ((0.25 * flow_rate) * (sq * h) * (gx * gx + gy * gy) + ext_e[now, here, :])
                    ext_d[now, here, :] = jnp.minimum(d, diff_cap)
                    ext_g[now, here, :] = right - s

        def h_rows(r, size):
            for at in range(r, r + size, 8):
                here, up, down = (slice(at + o, at + o + 8) for o in (0, -1, 1))
                edge = pltpu.roll(ext_d[1:2, here, :] * s_ref[1:2, here, :], LANES - 1, 2)
                for j in range(1, tiles + 1, GROUP):
                    now, later = (slice(j + o, j + o + GROUP) for o in (0, 1))
                    s, d = s_ref[now, here, :], ext_d[now, here, :]
                    right = pltpu.roll(jnp.where(first_lane, ext_d[later, here, :], d), LANES - 1, 2)
                    flux = (right + d) * ext_g[now, here, :]
                    sooner = jnp.concatenate([edge, flux[:-1]], axis=0)
                    edge = flux[-1:]
                    div = (ext_d[now, down, :] + d) * (s_ref[now, down, :] - s)
                    div += (ext_d[now, up, :] + d) * (s_ref[now, up, :] - s)
                    div += flux - pltpu.roll(jnp.where(last_lane, sooner, flux), 1, 2)
                    h = jnp.maximum(ext_h[now, here, :] + ((0.5 * time_step) * div + ext_m[now, here, :]), 0.0)
                    ext_h[now, here, :] = h
                    if t < STEPS:
                        s_new[now, here, :] = ext_b[now, here, :] + h

        sweep(lo_h - 1, 3 * rows - lo_h + 1, d_rows)
        sweep(lo_h, 3 * rows - lo_h, h_rows)

    for j in range(tiles):
        final_ref[:, lanes(j)] = ext_h[j + 1, mid, :]
    gives[1].start()
    gives[0].wait()
    gives[1].wait()


def per_device(n, mode_fields, coeff, eigen, map_friction, bed, smb, thickness):
    rows, cols = map_friction.shape
    mode_dev = mode_fields.shape[0]
    B = n // 4
    modes = coeff.shape[0]
    anywhere = pl.BlockSpec(memory_space=pl.ANY)
    strip = (rows, cols)
    ext = (cols // LANES + 2, 3 * rows + 2 * PAD, LANES)
    bf = jnp.bfloat16
    dma = pltpu.SemaphoreType.DMA
    return pl.pallas_call(
        functools.partial(kernel, n),
        out_shape=(jax.ShapeDtypeStruct(strip, F32),) * 2,
        in_specs=[anywhere] * 7,
        out_specs=(anywhere, anywhere),
        scratch_shapes=[
            pltpu.VMEM((1, modes), F32),
            pltpu.VMEM((1, modes), F32),
        ] + [pltpu.VMEM(strip, F32)] * 6 + [
            dma((6,)),
            dma((2,)),
            pltpu.VMEM((mode_dev, n * rows, cols), bf),
            pltpu.VMEM((2 * B,) + strip, F32),
            pltpu.VMEM((2 * B,) + strip, F32),
            pltpu.VMEM((2 * B,) + strip, F32),
            pltpu.VMEM((B,) + strip, WIRE),
            pltpu.VMEM((B,) + strip, WIRE),
            pltpu.VMEM((B,) + strip, WIRE),
            pltpu.VMEM((B,) + strip, WIRE),
            pltpu.VMEM(strip, F32),
            pltpu.VMEM((3,) + strip, bf),
            pltpu.VMEM((2, 3) + strip, bf),
            pltpu.VMEM(strip, bf),
            pltpu.VMEM((2,) + strip, bf),
        ] + [pltpu.VMEM(ext, F32)] * 8 + [
            dma((n,)), dma((2 * B,)), dma((2 * B,)), dma((B,)), dma((B,)), dma((B,)), dma((B,)), dma((4,)), dma((4,)),
        ],
        compiler_params=pltpu.CompilerParams(collective_id=0, has_side_effects=True, vmem_limit_bytes=60 * 2**20),
        name="posterior_ice",
    )(coeff.reshape(1, modes), eigen.reshape(1, modes), map_friction, bed, smb, thickness, mode_fields)


def solution(mesh):
    n = mesh.shape["modes"]
    return jax.shard_map(
        functools.partial(per_device, n),
        mesh=mesh,
        in_specs=(
            P(("groups", "modes"), None, None),
            P("groups"),
            P("groups"),
            P(("groups", "modes"), None),
            P(("groups", "modes"), None),
            P(("groups", "modes"), None),
            P(("groups", "modes"), None),
        ),
        out_specs=(P(("groups", "modes"), None), P(("groups", "modes"), None)),
        check_vma=False,
    )
```
